256 devices in a mesh: guide: 2 (over core), batch: 4 (over x), tensor: 32 (over z, y).
Axes of the slice: x: 4, y: 4, z: 8, core: 2. Of those that a mesh axis runs over, the one named last changes fastest.
Arguments:
- hidden_new: bfloat16 [2, 512, 2048], P('guide', ('batch', 'tensor')), may hold values from -6 to 6
- stored_rows: bfloat16 [2, 512, 24, 2048], P('guide', ('batch', 'tensor')), may hold values from -6 to 6
- key_cache: bfloat16 [2, 512, 288, 512], P('guide', ('batch', 'tensor')), as said below
- value_cache: bfloat16 [2, 512, 288, 512], P('guide', ('batch', 'tensor')), may hold values from -6 to 6
- lengths: int32 [2, 512], P('guide', ('batch', 'tensor')), may hold values from 72 to 287, as said below
- recompute_blocks: int32 [2, 512, 2], P('guide', ('batch', 'tensor')), may hold values from 0 to 22, as said below
- prefill_flags: int32 [512], P(('batch', 'tensor')), may hold values 0 or 1
- guidance: int32 [2], replicated, may hold values from 2 to 15
- attn_gain: float32 [2048], replicated, may hold values from 0.5 to 1.5
- query_gain: float32 [64], replicated, may hold values from 0.5 to 2
- key_gain: float32 [64], replicated, may hold values from 0.5 to 1.5
- final_gain: float32 [2048], replicated, may hold values from 0.5 to 1.5
- w_query: bfloat16 [2048, 2048], P(None, 'tensor'), may hold values from -0.125 to 0.125
- w_key: bfloat16 [2048, 512], P(None, 'tensor'), may hold values from -0.125 to 0.125
- w_value: bfloat16 [2048, 512], P(None, 'tensor'), may hold values from -0.125 to 0.125
- w_out: bfloat16 [2048, 2048], P('tensor'), may hold values from -0.125 to 0.125
- w_vocab: bfloat16 [2048, 65536], P(None, ('guide', 'batch', 'tensor')), may hold values from -0.125 to 0.125
Outputs:
- hidden_out: bfloat16 [2, 512, 2048], P('guide', ('batch', 'tensor'))
- key_out: bfloat16 [2, 512, 288, 512], P('guide', ('batch', 'tensor'))
- value_out: bfloat16 [2, 512, 288, 512], P('guide', ('batch', 'tensor'))
- guided: float32 [512, 65536], P(None, ('guide', 'batch', 'tensor'))
The draws below stay inside these ranges and needn't reach their ends.
Inputs may be any that keep to these rules, and one draw needn't show every extreme that they name: Each request's new token is written to cache row lengths, so lengths stay below 288; some request has 287 cached rows. `recompute_blocks`: the 2 block numbers of a request are different and each block lies wholly below that request's length. `key_cache`: finite values.
All inputs are finite; a program needn't handle non-finite values. No bound on the sum of `prefill_flags` on one device may be relied on, other than what follows from the above.
Results may differ from the reference program's by a relative error of at most 0.02.
Values may be sent and summed in bfloat16 or wider, within the bound.
No kernel may reach another device: no remote copies, remote signals or barrier semaphores. Data moves between devices by JAX's collectives and lax.ppermute only.
A program may use at most 128 MiB of HBM per device.

```python
import math
import jax
import jax.numpy as jnp
from jax import lax

D = 2048
H = 32
KVH = 8
HD = 64
V = 65536
CTX = 288
BLK = 12
NRB = 2
R = 512
NREC = 24
N_TENSOR = 32


def draw_plan(key):
    base_key = jax.random.fold_in(key, 11)
    key_len, key_spot, key_order = jax.random.split(base_key, 3)
    lowest = max(NRB * BLK, CTX // 4)
    drawn = jax.random.randint(key_len, (2 * R,), lowest, CTX)
    spot = jax.random.randint(key_spot, (), 0, 2 * R)
    drawn = jnp.where(jnp.arange(2 * R) == spot, CTX - 1, drawn).reshape(2, R)
    block_count = CTX // BLK
    ranks = jax.random.randint(key_order, (2, R, block_count), 0, 2 ** 20) * 64 + jnp.arange(block_count)
    usable = drawn[:, :, None] // BLK
    ranks = jnp.where(jnp.arange(block_count) < usable, ranks, ranks + 2 ** 28)
    order = jnp.argsort(ranks, axis=-1, stable=True)
    return (drawn.astype(jnp.int32), order[:, :, :NRB].astype(jnp.int32))


def draw_lengths(key, part):
    return draw_plan(key)[0]


def draw_recompute_blocks(key, part):
    return draw_plan(key)[1]


def draw_key_cache(key, part):
    key_base = jax.random.fold_in(jax.random.fold_in(key, 23), 0)
    base_vals = jnp.clip(jax.random.normal(key_base, (2, R, CTX, KVH * HD), jnp.float32), -6.0, 6.0)
    return base_vals.astype(jnp.bfloat16)


def place_ends(entries, stream_key, least, top_value):
    index_at = [jax.random.randint(jax.random.fold_in(stream_key, axis), (), 0, length) for axis, length in enumerate(entries.shape)]
    widest = entries.shape.index(max(entries.shape))
    neighbour = index_at[:widest] + [(index_at[widest] + 1) % entries.shape[widest]] + index_at[widest + 1:]
    return entries.at[tuple(index_at)].set(least).at[tuple(neighbour)].set(top_value)


def shard_levels(key, dims, pieces, low, high):
    gain = 1.0
    for dim, blocks in pieces:
        steps = jax.random.uniform(jax.random.fold_in(jax.random.fold_in(key, 6), dim), (blocks,), jnp.float32, low / len(pieces), high / len(pieces))
        gain = gain * jnp.repeat(jnp.exp(steps), dims[dim] // blocks).reshape((-1,) + (1,) * (len(dims) - 1 - dim))
    return gain


def noise(rng, dims, deviation, reach, shards=(), kind=jnp.bfloat16):
    factor_of = shard_levels(rng, dims, shards, -0.22, 0.18) if shards else 1.0
    values = jax.random.normal(rng, dims, jnp.float32) * deviation * factor_of
    return jnp.minimum(jnp.maximum(values, -reach), reach).astype(kind)


def setup_inputs(seed: int = 0) -> dict:
    streams_of = jax.random.split(jax.random.key(seed), 18)
    hidden_new = noise(streams_of[0], (2, R, D), 1.0, 6.0, ((0, 2), (1, 128)))
    stored_rows = noise(streams_of[1], (2, R, NREC, D), 1.0, 6.0, ((0, 2), (1, 128)))
    key_cache = draw_key_cache(jax.random.fold_in(streams_of[17], 71), 0)
    value_cache = noise(streams_of[3], (2, R, CTX, KVH * HD), 1.0, 6.0, ((0, 2), (1, 128)))
    lengths = draw_lengths(jax.random.fold_in(streams_of[17], 71), 0)
    recompute_blocks = draw_recompute_blocks(jax.random.fold_in(streams_of[17], 71), 0)
    prefill_flags = place_ends((jax.random.randint(streams_of[6], (R,), 0, 8) < 1).astype(jnp.int32), jax.random.fold_in(streams_of[6], 1), 0, 1)
    guidance = jax.random.randint(streams_of[7], (2,), 2, 16).astype(jnp.int32)
    attn_gain = jnp.clip(1.0 + 0.1 * jax.random.normal(streams_of[8], (D,), jnp.float32), 0.5, 1.5)
    query_gain = jnp.clip(jnp.exp(jax.random.uniform(streams_of[9], (HD,), jnp.float32, math.log(0.5), math.log(2.0))), 0.5, 2.0)
    key_gain = jnp.clip(1.0 + 0.1 * jax.random.normal(streams_of[10], (HD,), jnp.float32), 0.5, 1.5)
    final_gain = jnp.clip(1.0 + 0.1 * jax.random.normal(streams_of[11], (D,), jnp.float32), 0.5, 1.5)
    w_query = noise(streams_of[12], (D, H * HD), D ** -0.5, 0.125, ((1, 32),))
    w_key = noise(streams_of[13], (D, KVH * HD), D ** -0.5, 0.125, ((1, 32),))
    w_value = noise(streams_of[14], (D, KVH * HD), D ** -0.5, 0.125, ((1, 32),))
    w_out = noise(streams_of[15], (H * HD, D), (H * HD) ** -0.5, 0.125, ((0, 32),))
    w_vocab = noise(streams_of[16], (D, V), D ** -0.5, 0.125, ((1, 256),))
    return dict(hidden_new=hidden_new, stored_rows=stored_rows, key_cache=key_cache, value_cache=value_cache, lengths=lengths, recompute_blocks=recompute_blocks, prefill_flags=prefill_flags, guidance=guidance, attn_gain=attn_gain, query_gain=query_gain, key_gain=key_gain, final_gain=final_gain, w_query=w_query, w_key=w_key, w_value=w_value, w_out=w_out, w_vocab=w_vocab)


def rms_rows(values, gain_row):
    widened = values.astype(jnp.float32)
    return widened * lax.rsqrt(lax.optimization_barrier(jnp.mean(widened * widened, axis=-1, keepdims=True)) + 1e-05) * gain_row

def head_rms(values, gain_row, head_width):
    old_shape = values.shape
    split_heads = values.reshape(old_shape[:-1] + (old_shape[-1] // head_width, head_width))
    normed = split_heads * lax.rsqrt(lax.optimization_barrier(jnp.mean(split_heads * split_heads, axis=-1, keepdims=True)) + 1e-05) * gain_row
    return normed.reshape(old_shape)

def reference(hidden_new, stored_rows, key_cache, value_cache, lengths, recompute_blocks, prefill_flags, guidance, attn_gain, query_gain, key_gain, final_gain, w_query, w_key, w_value, w_out, w_vocab):
    group_size = H // KVH
    score_scale = HD ** (-0.5)
    offsets = jnp.arange(NREC, dtype=jnp.int32)
    block_slot = offsets // BLK
    within_block = offsets % BLK
    columns = jnp.arange(CTX, dtype=jnp.int32)
    group_width = H * HD // N_TENSOR

    def one_request(inputs):
        token_row, stored, cache_keys, cache_values, length, blocks, flag = inputs
        normed_new = rms_rows(token_row[None, :], attn_gain).astype(jnp.bfloat16)
        normed_old = rms_rows(stored, attn_gain).astype(jnp.bfloat16)
        kv_rows = jnp.concatenate([normed_old, normed_new], axis=0)
        keys_raw = jnp.dot(kv_rows, w_key, preferred_element_type=jnp.float32).astype(jnp.bfloat16)
        keys_all = head_rms(keys_raw.astype(jnp.float32), key_gain, HD).astype(jnp.bfloat16)
        values_all = jnp.dot(kv_rows, w_value, preferred_element_type=jnp.float32).astype(jnp.bfloat16)
        query_row = head_rms(jnp.dot(normed_new, w_query, preferred_element_type=jnp.float32), query_gain, HD).astype(jnp.bfloat16)
        positions = (blocks[block_slot] * BLK + within_block).astype(jnp.int32)
        new_keys = cache_keys.at[positions].set(keys_all[:NREC]).at[length].set(keys_all[NREC])
        new_values = cache_values.at[positions].set(values_all[:NREC]).at[length].set(values_all[NREC])
        query_heads = query_row.reshape(KVH, group_size, HD).astype(jnp.float32)
        key_heads = new_keys.reshape(CTX, KVH, HD).astype(jnp.float32)
        scores = jnp.einsum('kgd,jkd->kgj', query_heads, key_heads) * score_scale
        visible = (columns < length) & (flag == 0) | (columns == length)
        scores = jnp.where(visible, scores, -1e+30)
        row_max = lax.optimization_barrier(jnp.max(scores, axis=-1, keepdims=True))
        powers = jnp.exp(scores - row_max)
        attn_probs = (powers / lax.optimization_barrier(jnp.sum(powers, axis=-1, keepdims=True))).astype(jnp.bfloat16)
        value_heads = new_values.reshape(CTX, KVH, HD).astype(jnp.float32)
        attended = jnp.einsum('kgj,jkd->kgd', attn_probs.astype(jnp.float32), value_heads).astype(jnp.bfloat16)
        return (attended.reshape(H * HD), new_keys, new_values)
    weight = guidance[0].astype(jnp.float32) / guidance[1].astype(jnp.float32)
    residuals = []
    key_parts = []
    value_parts = []
    logit_sides = []
    for guide_side in range(2):
        attended, new_keys, new_values = lax.map(one_request, (hidden_new[guide_side], stored_rows[guide_side], key_cache[guide_side], value_cache[guide_side], lengths[guide_side], recompute_blocks[guide_side], prefill_flags))
        projected = jnp.zeros((R, D), jnp.float32)
        for group in range(N_TENSOR):
            part_in = attended[:, group * group_width:(group + 1) * group_width]
            part_w = w_out[group * group_width:(group + 1) * group_width, :]
            head_partial = jnp.dot(part_in, part_w, preferred_element_type=jnp.float32).astype(jnp.bfloat16)
            projected = projected + head_partial.astype(jnp.float32)
        residual = (hidden_new[guide_side].astype(jnp.float32) + projected).astype(jnp.bfloat16)
        normed_final = rms_rows(residual, final_gain).astype(jnp.bfloat16)
        logits = jnp.dot(normed_final, w_vocab, preferred_element_type=jnp.float32).astype(jnp.bfloat16)
        residuals.append(residual)
        key_parts.append(new_keys)
        value_parts.append(new_values)
        logit_sides.append(logits)
    cond_logits = logit_sides[0].astype(jnp.float32)
    uncond_logits = logit_sides[1].astype(jnp.float32)
    guided = uncond_logits + weight * (cond_logits - uncond_logits)
    return (jnp.stack(residuals), jnp.stack(key_parts), jnp.stack(value_parts), guided)
```

```python
import jax
import jax.numpy as jnp
from jax import lax
from jax.experimental import pallas as pl
from jax.experimental.pallas import tpu as pltpu
from jax.sharding import Mesh, PartitionSpec as P

BF = jnp.bfloat16
F32 = jnp.float32
NT = (((1,), (1,)), ((), ()))


def rms_rows(values, gain_row):
    widened = values.astype(F32)
    return (
        widened * lax.rsqrt(jnp.mean(widened * widened, axis=-1, keepdims=True) + 1e-05) * gain_row
    )


def spread(rows, axes, count):
    sent = jnp.broadcast_to(rows[None], (count,) + rows.shape)
    return lax.all_to_all(sent, axes, split_axis=0, concat_axis=0, tiled=True)


def swap_guide(values):
    return lax.ppermute(values, "guide", [(0, 1), (1, 0)])


def attend_body(
    scal_ref, kv_ref, q_ref, kgain_ref, kc_ref, vc_ref, ko_ref, vo_ref, att_ref, k_all, v_all
):
    r = pl.program_id(0)
    nrow = k_all.shape[0]
    ctx, width = kc_ref.shape[1], kc_ref.shape[2]
    old = 96

    @pl.when(r == 0)
    def _():
        m = lax.broadcasted_iota(jnp.int32, (width, width), 0)
        c = lax.broadcasted_iota(jnp.int32, (width, width), 1)
        src = ((c // 4) % 4) * 128 + (c // 16) * 4 + c % 4
        perm = (m == src).astype(F32).astype(BF)
        k_in = jnp.concatenate([kv_ref[i] for i in range(4)], axis=1)
        v_in = jnp.concatenate([kv_ref[i] for i in range(4, 8)], axis=1)
        k_raw = jnp.dot(k_in, perm, preferred_element_type=F32)
        v_all[...] = jnp.dot(v_in, perm, preferred_element_type=F32).astype(BF)
        same = (m // 64 == c // 64).astype(F32)
        mean = jnp.dot(
            k_raw * k_raw, same, preferred_element_type=F32, precision=lax.Precision.HIGHEST
        ) * (1.0 / 64)
        k_all[...] = (k_raw * lax.rsqrt(mean + 1e-05) * kgain_ref[...]).astype(BF)

    length = scal_ref[0, r]
    b0 = scal_ref[1, r] * 12
    b1 = scal_ref[2, r] * 12
    flag = scal_ref[3, r]

    i = lax.broadcasted_iota(jnp.int32, (1, nrow), 1)
    w = i - r * 24
    pos = jnp.where(w < 12, b0 + w, b1 + w - 12)
    pos = jnp.where((w >= 0) & (w < 24) & (i < old), pos, -1)
    pos = jnp.where(i == old + r, length, pos)
    j = lax.broadcasted_iota(jnp.int32, (ctx, nrow), 0)
    sel = (j == pos).astype(F32).astype(BF)
    jr = lax.broadcasted_iota(jnp.int32, (ctx, 1), 0)
    hit = (
        ((jr >= b0) & (jr < b0 + 12)) | ((jr >= b1) & (jr < b1 + 12)) | (jr == length)
    )
    new_k = jnp.dot(sel, k_all[...], preferred_element_type=F32)
    new_k = jnp.where(hit, new_k, kc_ref[0].astype(F32)).astype(BF)
    ko_ref[0] = new_k
    new_v = jnp.dot(sel, v_all[...], preferred_element_type=F32)
    new_v = jnp.where(hit, new_v, vc_ref[0].astype(F32)).astype(BF)
    vo_ref[0] = new_v

    heads = q_ref.shape[0]
    lq = lax.broadcasted_iota(jnp.int32, (q_ref.shape[1], width), 0)
    cq = lax.broadcasted_iota(jnp.int32, (q_ref.shape[1], width), 1)
    tile = (lq == r * 64 + cq % 64).astype(F32).astype(BF)
    h = lax.broadcasted_iota(jnp.int32, (heads, width), 0)
    ch = lax.broadcasted_iota(jnp.int32, (heads, width), 1)
    own = h // 4 == ch // 64
    q_wide = jnp.where(own, jnp.dot(q_ref[...], tile, preferred_element_type=F32), 0.0).astype(BF)
    scores = lax.dot_general(q_wide, new_k, NT, preferred_element_type=F32) * 0.125
    col = lax.broadcasted_iota(jnp.int32, (heads, ctx), 1)
    visible = ((col < length) & (flag == 0)) | (col == length)
    scores = jnp.where(visible, scores, -1e30)
    top = jnp.max(scores, axis=-1, keepdims=True)
    powers = jnp.exp(scores - top)
    probs = (powers / jnp.sum(powers, axis=-1, keepdims=True)).astype(BF)
    wide = jnp.where(own, jnp.dot(probs, new_v, preferred_element_type=F32), 0.0).astype(BF)
    gh = lax.broadcasted_iota(jnp.int32, (4, heads), 0)
    hh = lax.broadcasted_iota(jnp.int32, (4, heads), 1)
    pick = (hh % 4 == gh).astype(F32).astype(BF)
    att_ref[0] = jnp.dot(pick, wide, preferred_element_type=F32).astype(BF)


def attend(scal, kv_back, q_all, kgain, key_cache, value_cache):
    n, ctx, width = key_cache.shape
    nrow = kv_back.shape[1]
    whole = lambda a: pl.BlockSpec(a.shape, lambda r, s: (0,) * a.ndim)
    one = pl.BlockSpec((1, ctx, width), lambda r, s: (r, 0, 0))
    return pl.pallas_call(
        attend_body,
        grid_spec=pltpu.PrefetchScalarGridSpec(
            num_scalar_prefetch=1,
            grid=(n,),
            in_specs=[whole(kv_back), whole(q_all), whole(kgain), one, one],
            out_specs=[one, one, pl.BlockSpec((1, 4, width), lambda r, s: (r, 0, 0))],
            scratch_shapes=[pltpu.VMEM((nrow, width), BF), pltpu.VMEM((nrow, width), BF)],
        ),
        out_shape=[
            jax.ShapeDtypeStruct(key_cache.shape, BF),
            jax.ShapeDtypeStruct(value_cache.shape, BF),
            jax.ShapeDtypeStruct((n, 4, width), BF),
        ],
        compiler_params=pltpu.CompilerParams(vmem_limit_bytes=40 << 20),
        name="attend",
    )(scal, kv_back, q_all, kgain, key_cache, value_cache)


def local(
    hidden_new,
    stored_rows,
    key_cache,
    value_cache,
    lengths,
    recompute_blocks,
    prefill_flags,
    guidance,
    attn_gain,
    query_gain,
    key_gain,
    final_gain,
    w_query,
    w_key,
    w_value,
    w_out,
    w_vocab,
):
    width = hidden_new.shape[2]
    side = lax.axis_index("guide")
    eighth = side * 4 + lax.axis_index("batch")
    x_rows = hidden_new[0]
    normed_new = rms_rows(x_rows, attn_gain).astype(BF)

    kv_cols = jnp.concatenate([w_key.T, w_value.T], axis=0)
    kv_eighth = lax.dynamic_slice_in_dim(kv_cols, eighth * 4, 4, 0)
    got = spread(jnp.concatenate([kv_eighth, normed_new], axis=0), ("z", "y"), 32)
    kv_w = got[:, :4].reshape(128, width)

    normed_old = rms_rows(stored_rows[0], attn_gain).astype(BF).reshape(96, width)
    kv_rows = jnp.concatenate([normed_old, normed_new, jnp.zeros((4, width), BF)], axis=0)
    rows_mine = spread(kv_rows, "batch", 4)
    rows_other = swap_guide(rows_mine)
    dot_kv = lambda a: lax.dot_general(
        a.reshape(416, width), kv_w, NT, preferred_element_type=F32
    ).astype(BF).reshape(1, 4, 104, 128)
    kv_mine, kv_other = dot_kv(rows_mine), dot_kv(rows_other)
    kv_sent = jnp.where(
        side == 0,
        jnp.concatenate([kv_mine, kv_other], axis=0),
        jnp.concatenate([kv_other, kv_mine], axis=0),
    ).reshape(8, 104, 128)
    kv_back = lax.all_to_all(
        kv_sent, ("guide", "batch"), split_axis=0, concat_axis=0, tiled=True
    )

    q_raw = jnp.dot(got.reshape(256, width), w_query, preferred_element_type=F32)
    q_raw = q_raw.reshape(32, 8, 64)[:, 4:]
    q_part = rms_rows(q_raw, query_gain).astype(BF).reshape(32, 2, 128)
    q_all = lax.all_to_all(q_part, ("z", "y"), split_axis=0, concat_axis=0, tiled=True)
    q_all = q_all.reshape(32, 256)

    scal = jnp.concatenate(
        [lengths, recompute_blocks[0].T, prefill_flags[None]], axis=0
    )
    kgain = jnp.tile(key_gain, 8)[None]
    new_keys, new_values, att = attend(scal, kv_back, q_all, kgain, key_cache[0], value_cache[0])

    wo_eighth = lax.dynamic_slice_in_dim(w_out, eighth * 256, 256, 1)
    wo = spread(wo_eighth, ("y", "z"), 32).reshape(width, 256)
    att_all = spread(att.reshape(16, 512), ("guide", "batch"), 8).reshape(32, width)
    proj = jnp.dot(att_all, wo, preferred_element_type=F32).reshape(8, 4, 256)
    proj = lax.all_to_all(proj, ("guide", "batch"), split_axis=0, concat_axis=0, tiled=True)
    projected = proj.transpose(1, 0, 2).reshape(4, width)
    residual = (x_rows.astype(F32) + projected).astype(BF)

    weight = guidance[0].astype(F32) / guidance[1].astype(F32)
    final = rms_rows(residual, final_gain) * jnp.where(side == 0, weight, 1.0 - weight)
    half = width // 2
    keep = lax.dynamic_slice_in_dim(final, side * half, half, 1)
    give = lax.dynamic_slice_in_dim(final, (1 - side) * half, half, 1)
    both = (keep + swap_guide(give)).astype(BF)
    both = spread(both, "z", 8).reshape(32, half)
    rows_half = spread(both, ("batch", "y"), 16).reshape(512, half)
    rows_rest = swap_guide(rows_half)
    w_half = lax.dynamic_slice_in_dim(w_vocab, side * half, half, 0)
    w_rest = lax.dynamic_slice_in_dim(w_vocab, (1 - side) * half, half, 0)
    guided = jnp.dot(rows_half, w_half, preferred_element_type=F32) + jnp.dot(
        rows_rest, w_rest, preferred_element_type=F32
    )
    guided = guided.reshape(4, 4, 8, 4, 256).transpose(0, 2, 1, 3, 4).reshape(512, 256)
    return (residual[None], new_keys[None], new_values[None], guided)


def solution(mesh):
    mesh = Mesh(mesh.devices.reshape(2, 4, 8, 4), ("guide", "batch", "z", "y"))
    tensor = ("z", "y")
    rows = ("batch", "z", "y")
    in_specs = (
        P("guide", rows, None),
        P("guide", rows, None, None),
        P("guide", rows, None, None),
        P("guide", rows, None, None),
        P("guide", rows),
        P("guide", rows, None),
        P(rows),
        P(),
        P(),
        P(),
        P(),
        P(),
        P(None, tensor),
        P(None, tensor),
        P(None, tensor),
        P(tensor, None),
        P(None, ("guide",) + rows),
    )
    out_specs = (
        P("guide", rows, None),
        P("guide", rows, None, None),
        P("guide", rows, None, None),
        P(None, ("guide",) + rows),
    )
    return jax.shard_map(local, mesh=mesh, in_specs=in_specs, out_specs=out_specs, check_vma=False)
```
